1024 devices in a mesh: expert: 64 (over y, x), dp: 16 (over z, core).
Axes of the slice: x: 8, y: 8, z: 8, core: 2. Of those that a mesh axis runs over, the one named last changes fastest.
Arguments:
- tokens: bfloat16 [16384, 2048], P(('dp', 'expert')), may hold values from -6 to 6
- cotangent: bfloat16 [16384, 8, 384], P(('dp', 'expert')), may hold values from -1 to 1
- expert_ids: int32 [16384, 8], P(('dp', 'expert')), may hold values from 0 to 31, all different within a row; in each aligned block of 16 rows (0 to 15, 16 to 31, ...) at most 5 rows name the same one
- placement: int32 [64], replicated, may hold values from 0 to 31, as said below
- master: float32 [32, 1572864], P(None, ('dp', 'expert')), may hold values from -0.125 to 0.125
- first_moment: float32 [32, 1572864], P(None, ('dp', 'expert')), may hold values from -12 to 12
- second_moment: float32 [32, 1572864], P(None, ('dp', 'expert')), may hold values from 1 to 30
Outputs:
- new_master: float32 [32, 1572864], P(None, ('dp', 'expert'))
- new_first: float32 [32, 1572864], P(None, ('dp', 'expert'))
- new_second: float32 [32, 1572864], P(None, ('dp', 'expert'))
- replica_grad: float32 [64, 384, 4096], P('expert', 'dp')
The draws below stay inside these ranges and needn't reach their ends.
Inputs may be any that keep to these rules, and one draw needn't show every extreme that they name: `expert_ids`: among the tokens of one device no expert is named more than 5 times; some device names some expert exactly 5 times. `placement`: every one of the 32 experts holds at least one of the 64 slots.
All inputs are finite; a program needn't handle non-finite values.
Results may differ from the reference program's by a relative error of at most 0.017.
Values may be sent and summed in bfloat16 or wider, within the bound.
No kernel may reach another device: no remote copies, remote signals or barrier semaphores. Data moves between devices by JAX's collectives and lax.ppermute only.
A program may use at most 64 MiB of HBM per device.

```python
import math
import jax
import jax.numpy as jnp
import numpy as np
from jax import lax

D = 2048
FF = 384
EXP = 32
TOP = 8
TOK_DEV = 16
MOST = 5
SLOTS = 64
TOKENS = 16384
N_EXPERT = 64
N_DP = 16


def draw_placement(key, part):
    first_key = jax.random.fold_in(key, 11)
    second_key = jax.random.fold_in(key, 12)
    label_key = jax.random.fold_in(key, 13)
    order_key = jax.random.fold_in(key, 14)
    first_pick = jax.random.randint(first_key, (SLOTS - EXP,), 0, EXP)
    second_pick = jax.random.randint(second_key, (SLOTS - EXP,), 0, EXP)
    extra = jnp.minimum(first_pick, second_pick)
    base = jnp.concatenate([jnp.arange(EXP, dtype=jnp.int32), extra.astype(jnp.int32)])
    relabel = jax.random.permutation(label_key, EXP).astype(jnp.int32)
    labelled = relabel[base]
    order = jax.random.permutation(order_key, SLOTS).astype(jnp.int32)
    return labelled[order].astype(jnp.int32)


def level_of(rng, dims, split, smallest, high):
    def one(axis_at, shards_of):
        steps = jax.random.uniform(jax.random.fold_in(jax.random.fold_in(rng, 6), axis_at), (shards_of,), jnp.float32, smallest / len(split), high / len(split))
        return jnp.repeat(jnp.exp(steps), dims[axis_at] // shards_of).reshape((-1,) + (1,) * (len(dims) - axis_at - 1))

    level = one(*split[0])
    for cut in split[1:]:
        level = level * one(*cut)
    return level


def shared_out(own_key, own, number, rows, amount, top, most, lean):
    sequence = jax.random.permutation(own_key, amount)
    crowded, usual = load_shares(amount, rows * top, most, lean, True), load_shares(amount, rows * top, most, lean, False)
    places = jnp.arange(amount)

    def named(tallies, turn):
        used = int((tallies > 0).sum())
        fixed = max(1, used // 4)
        moved = fixed + (places - fixed + turn * (used - fixed)) % max(1, amount - fixed)
        return jnp.zeros((amount,), jnp.int32).at[sequence[jnp.where(places < fixed, places, moved)]].set(jnp.asarray(tallies, jnp.int32))

    tallies = jnp.where(number % 4 == 0, named(crowded, number // 4), named(usual, number - number // 4 - 1))
    mixed = jax.random.permutation(jax.random.fold_in(own, 3), amount)
    giver, sink = mixed[0:amount // 2 * 2:2], mixed[1:amount // 2 * 2:2]
    margin = jnp.minimum(tallies[giver] - 1, most - tallies[sink]) // 2
    margin = jnp.where((giver == sequence[0]) | (sink == sequence[0]) | (tallies[sink] == 0), 0, jnp.maximum(margin, 0))
    moved = jax.random.randint(jax.random.fold_in(own, 4), (amount // 2,), 0, 1 << 20) % (margin + 1)
    tallies = tallies.at[giver].add(-moved).at[sink].add(moved)
    members = jnp.searchsorted(jnp.cumsum(tallies), jnp.arange(rows * top), side="right").astype(jnp.int32)
    listing = members.reshape(top, rows).T
    listing = listing[jax.random.permutation(jax.random.fold_in(own, 1), rows)]
    turn = jax.random.randint(jax.random.fold_in(own, 2), (rows, 1), 0, top)
    return jnp.take_along_axis(listing, (jnp.arange(top)[None, :] + turn) % top, axis=1)


def load_shares(amount, total, limit, skew, full):
    portions = [(1 << 20) // math.isqrt(standing ** skew) + 1 for standing in range(1, amount + 1)]
    largest = limit if full else min(limit, max(-(-total // amount), total * portions[0] // sum(portions)))
    least = 1 if total - largest >= amount - 1 else 0
    given, rest = [largest] + [least] * (amount - 1), total - largest - least * (amount - 1)
    while rest > 0:
        candidates = [i for i in range(1, amount) if given[i] < largest] or [i for i in range(1, amount) if given[i] < limit]
        mass, remaining = sum([portions[i] for i in candidates]), rest
        for i in candidates:
            addition = min(limit - given[i], max(1, remaining * portions[i] // mass), rest)
            given[i] = given[i] + addition
            rest = rest - addition
    return np.array(given)


def scatter_about(key, shape, scale, limit, split=(), kind=jnp.bfloat16):
    array = scale * jax.random.normal(key, shape, jnp.float32)
    if split:
        array = array * level_of(key, shape, split, -0.22, 0.18)
    return jnp.clip(array, -limit, limit).astype(kind)


def setup_inputs(seed: int = 0) -> dict:
    arg_keys = jax.random.split(jax.random.key(seed), 8)
    tokens = scatter_about(arg_keys[0], (TOKENS, D), 1.0, 6.0, ((0, 1024),))
    cotangent = scatter_about(arg_keys[1], (TOKENS, TOP, FF), 0.125, 1.0, ((0, 1024),))
    expert_ids_keys = jax.random.split(jax.random.fold_in(arg_keys[2], 1), TOKENS // TOK_DEV)
    expert_ids_turns = jax.random.permutation(jax.random.fold_in(arg_keys[2], 3), TOKENS // TOK_DEV)
    expert_ids = jax.vmap(lambda own, number: shared_out(jax.random.fold_in(arg_keys[2], 2), own, number, TOK_DEV, EXP, TOP, MOST, 2))(expert_ids_keys, expert_ids_turns).reshape((TOKENS, TOP))
    placement = draw_placement(jax.random.fold_in(arg_keys[7], 71), 0)
    master = scatter_about(arg_keys[4], (EXP, FF * 2 * D), D ** -0.5, 0.125, ((1, 1024),), jnp.float32)
    first_moment = scatter_about(arg_keys[5], (EXP, FF * 2 * D), 2.0, 12.0, ((1, 1024),), jnp.float32)
    second_moment = jnp.clip(jnp.exp(math.log(30.0) - 3.4011974 * jax.random.uniform(arg_keys[6], (EXP, FF * 2 * D), jnp.float32) ** level_of(arg_keys[6], (EXP, FF * 2 * D), ((1, 1024),), -0.2, 0.2)), 1.0, 30.0)
    return {"tokens": tokens, "cotangent": cotangent, "expert_ids": expert_ids, "placement": placement, "master": master, "first_moment": first_moment, "second_moment": second_moment}


beta_first = 0.9
beta_second = 0.95
learning_rate = 0.01
decay_rate = 0.1
epsilon = 1e-08
adam_steps = 20.0

def adamw_update(master, first_moment, second_moment, grads):
    new_first = beta_first * first_moment + (1.0 - beta_first) * grads
    new_second = beta_second * second_moment + (1.0 - beta_second) * grads * grads
    corr_first = 1.0 - beta_first ** adam_steps
    corr_second = 1.0 - beta_second ** adam_steps
    update = new_first / corr_first / (jnp.sqrt(new_second / corr_second) + epsilon) + decay_rate * master
    return (master - learning_rate * update, new_first, new_second)

def swiglu_grads(rows_x, rows_dh, w_gate, w_up):
    gate_value = jnp.dot(rows_x, w_gate.T, preferred_element_type=jnp.float32)
    up_value = jnp.dot(rows_x, w_up.T, preferred_element_type=jnp.float32)
    sigmoid_value = jax.nn.sigmoid(gate_value)
    activation = gate_value * sigmoid_value
    derivative = sigmoid_value * (1.0 + gate_value * (1.0 - sigmoid_value))
    d_gate = (rows_dh * up_value * derivative).astype(jnp.bfloat16)
    d_up = (rows_dh * activation).astype(jnp.bfloat16)
    grad_gate = jnp.dot(d_gate.T, rows_x, preferred_element_type=jnp.float32)
    grad_up = jnp.dot(d_up.T, rows_x, preferred_element_type=jnp.float32)
    return jnp.concatenate([grad_gate, grad_up], axis=1)

def reference(tokens, cotangent, expert_ids, placement, master, first_moment, second_moment):
    assigned = TOK_DEV * TOP
    token_blocks = tokens.reshape(N_DP, N_EXPERT, TOK_DEV, D)
    cot_blocks = cotangent.reshape(N_DP, N_EXPERT, assigned, FF)
    id_blocks = expert_ids.reshape(N_DP, N_EXPERT, assigned)
    expert_range = jnp.arange(EXP, dtype=jnp.int32)
    slot_range = jnp.arange(SLOTS, dtype=jnp.int32)
    replicas = lax.optimization_barrier(jnp.sum((placement[:, None] == expert_range[None, :]).astype(jnp.int32), axis=0))
    earlier_same = (slot_range[:, None] > slot_range[None, :]) & (placement[:, None] == placement[None, :])
    slot_rank = lax.optimization_barrier(jnp.sum(earlier_same.astype(jnp.int32), axis=1))
    expert_hot = id_blocks[..., None] == expert_range
    earlier = jnp.cumsum(expert_hot.astype(jnp.int32), axis=2) - 1
    position = lax.optimization_barrier(jnp.sum(jnp.where(expert_hot, earlier, 0), axis=3))
    weights = master.astype(jnp.bfloat16).reshape(EXP, FF, 2 * D)
    sources = jnp.arange(N_EXPERT, dtype=jnp.int32)
    capacity_range = jnp.arange(MOST, dtype=jnp.int32)

    def slot_step(grads, slot_index):
        expert_index = placement[slot_index]
        chosen = jnp.mod(sources, replicas[expert_index]) == slot_rank[slot_index]
        keep = (id_blocks == expert_index) & chosen[None, :, None]
        slot_rows = (keep[..., None] & (position[..., None] == capacity_range)).astype(jnp.float32)
        replica_weight = weights[expert_index]
        w_gate = replica_weight[:, :D]
        w_up = replica_weight[:, D:]

        def dp_step(total, dp_index):
            picks = slot_rows[dp_index]
            token_picks = lax.optimization_barrier(jnp.sum(picks.reshape(N_EXPERT, TOK_DEV, TOP, MOST), axis=2))
            rows_x = jnp.einsum('stm,std->smd', token_picks, token_blocks[dp_index].astype(jnp.float32))
            rows_x = rows_x.reshape(N_EXPERT * MOST, D).astype(jnp.bfloat16)
            rows_dh = jnp.einsum('sam,saf->smf', picks, cot_blocks[dp_index].astype(jnp.float32))
            rows_dh = rows_dh.reshape(N_EXPERT * MOST, FF).astype(jnp.bfloat16)
            term = swiglu_grads(rows_x, rows_dh, w_gate, w_up)
            rounded = lax.optimization_barrier(term.astype(jnp.bfloat16)).astype(jnp.float32)
            return (total + rounded, None)
        total, _ = lax.scan(dp_step, jnp.zeros((FF, 2 * D), jnp.float32), jnp.arange(N_DP, dtype=jnp.int32))
        return (grads.at[expert_index].add(total.reshape(FF * 2 * D)), total)
    grads, replica_grad = lax.scan(slot_step, jnp.zeros((EXP, FF * 2 * D), jnp.float32), slot_range)
    new_master, new_first, new_second = adamw_update(master, first_moment, second_moment, grads)
    return (new_master, new_first, new_second, replica_grad)
```

```python
import functools

import jax
import jax.numpy as jnp
from jax import lax
from jax.experimental import pallas as pl
from jax.experimental.pallas import tpu as pltpu
from jax.sharding import Mesh, PartitionSpec as P

MOST = 5
LANES = 128
CORES = 2


beta_first = 0.9
beta_second = 0.95
learning_rate = 0.01
decay_rate = 0.1
epsilon = 1e-08
adam_steps = 20.0


def adamw_update(master, first_moment, second_moment, grads):
    new_first = beta_first * first_moment + (1.0 - beta_first) * grads
    new_second = beta_second * second_moment + (1.0 - beta_second) * grads * grads
    corr_first = 1.0 - beta_first**adam_steps
    corr_second = 1.0 - beta_second**adam_steps
    update = (
        new_first / corr_first / (jnp.sqrt(new_second / corr_second) + epsilon)
        + decay_rate * master
    )
    return (master - learning_rate * update, new_first, new_second)


def grads_kernel(piece_rows, core, x_own, x_other, dh_own, dh_other, weights, out):
    f32, bf16 = jnp.float32, jnp.bfloat16
    units, width = weights.shape[0], weights.shape[1] // 2
    hidden = dh_own.shape[1]
    across = (((1,), (1,)), ((), ()))
    unit = lax.broadcasted_iota(jnp.int32, (units, hidden), 0)
    column = lax.broadcasted_iota(jnp.int32, (units, hidden), 1)
    piece = unit // piece_rows
    wanted = (piece * CORES + core[0]) * piece_rows + unit - piece * piece_rows
    choose = (column == wanted).astype(f32).astype(bf16)
    d_gates, d_ups = [], []
    for x_ref, dh_ref in ((x_own, dh_own), (x_other, dh_other)):
        rows = x_ref[...]
        dh = lax.dot_general(choose, dh_ref[...], across, preferred_element_type=f32)
        gate = lax.dot_general(weights[:, :width], rows, across, preferred_element_type=f32)
        up = lax.dot_general(weights[:, width:], rows, across, preferred_element_type=f32)
        sig = jax.nn.sigmoid(gate)
        d_gates.append((dh * up * (sig * (1.0 + gate * (1.0 - sig)))).astype(bf16))
        d_ups.append((dh * (gate * sig)).astype(bf16))
    tile = 512
    for half, parts in enumerate((d_gates, d_ups)):
        for start in range(0, width, tile):
            cols = slice(start, start + tile)
            total = jnp.dot(parts[0], x_own[:, cols], preferred_element_type=f32)
            total += jnp.dot(parts[1], x_other[:, cols], preferred_element_type=f32)
            out[:, half * width + start : half * width + start + tile] = total.astype(bf16)


def swiglu_grads(core, x_own, x_other, dh_own, dh_other, weights, piece_rows):
    vmem = pl.BlockSpec(memory_space=pltpu.VMEM)
    flops = 16 * x_own.shape[0] * weights.size // 2
    return pl.pallas_call(
        functools.partial(grads_kernel, piece_rows),
        out_shape=jax.ShapeDtypeStruct(weights.shape, jnp.bfloat16),
        in_specs=[pl.BlockSpec(memory_space=pltpu.SMEM)] + [vmem] * 5,
        out_specs=vmem,
        cost_estimate=pl.CostEstimate(flops=flops, bytes_accessed=8 << 20, transcendentals=0),
    )(core.reshape(1), x_own, x_other, dh_own, dh_other, weights)


def local(tokens, cotangent, expert_ids, placement, master, first_moment, second_moment):
    bf16, f32, i32 = jnp.bfloat16, jnp.float32, jnp.int32
    slots = lax.axis_size("expert")
    planes = lax.axis_size("z")
    source_index = lax.axis_index("expert")
    core = lax.axis_index("c")
    expert_count, shard_width = master.shape
    token_rows, width = tokens.shape
    top_count = expert_ids.shape[1]
    hidden = cotangent.shape[2]
    assigned = token_rows * top_count
    piece_rows = shard_width * slots // (2 * width)
    rows = slots * MOST
    expert_range = jnp.arange(expert_count, dtype=i32)
    slot_range = jnp.arange(slots, dtype=i32)

    slot_hot = placement[:, None] == expert_range[None, :]
    send_weight = jnp.dot(
        slot_hot.astype(bf16), master.astype(bf16), preferred_element_type=f32
    ).astype(bf16)
    send_weight = send_weight.reshape(slots, shard_width // LANES, LANES)
    recv_weight = lax.all_to_all(send_weight, "expert", split_axis=0, concat_axis=0, tiled=True)

    replicas = jnp.sum(slot_hot.astype(i32), axis=0)
    earlier_same = (slot_range[:, None] > slot_range[None, :]) & (
        placement[:, None] == placement[None, :]
    )
    slot_rank = jnp.sum(earlier_same.astype(i32), axis=1)
    wanted = jnp.mod(source_index, replicas)
    target_hot = slot_hot & (slot_rank[:, None] == wanted[None, :])
    target_slot = jnp.sum(jnp.where(target_hot, slot_range[:, None], 0), axis=0)
    flat_ids = expert_ids.reshape(assigned)
    expert_hot = flat_ids[:, None] == expert_range[None, :]
    copy_range = jnp.arange(assigned, dtype=i32)
    before = (copy_range[:, None] > copy_range[None, :]) & (flat_ids[:, None] == flat_ids[None, :])
    position = jnp.sum(before.astype(i32), axis=1)
    destination = jnp.sum(jnp.where(expert_hot, target_slot[None, :], 0), axis=1)
    send_row = destination * MOST + position
    row_match = jnp.arange(rows, dtype=i32)[:, None] == send_row[None, :]
    pick = row_match.astype(bf16)
    token_of = (copy_range[:, None] // top_count == jnp.arange(token_rows, dtype=i32)[None, :])
    token_pick = jnp.dot(pick, token_of.astype(bf16), preferred_element_type=f32).astype(bf16)
    send_x = jnp.dot(token_pick, tokens, preferred_element_type=f32).astype(bf16)
    send_dh = jnp.dot(
        pick, cotangent.reshape(assigned, hidden), preferred_element_type=f32
    ).astype(bf16)
    x_rows = MOST * width // LANES
    dh_rows = MOST * hidden // LANES
    spare = -(x_rows + dh_rows) % 16
    send = jnp.concatenate(
        [
            send_x.reshape(slots, x_rows, LANES),
            send_dh.reshape(slots, dh_rows, LANES),
            jnp.zeros((slots, spare, LANES), bf16),
        ],
        axis=1,
    )
    send, recv_weight = lax.optimization_barrier((send, recv_weight))
    recv = lax.all_to_all(send, "expert", split_axis=0, concat_axis=0, tiled=True)
    other = lax.ppermute(recv, "c", [(0, 1), (1, 0)])

    own_piece = recv_weight.reshape(piece_rows, 2 * width)
    replica = lax.all_gather(own_piece, "z", axis=0, tiled=True)

    group = MOST + 1

    def rows_of(block):
        wide = block.reshape(slots * group, width)
        dh = block[:, x_rows : x_rows + dh_rows].reshape(slots, MOST, hidden)
        dh = jnp.pad(dh, ((0, 0), (0, group - MOST), (0, 0))).reshape(slots * group, hidden)
        return wide, dh

    x_own, dh_own = rows_of(recv)
    x_other, dh_other = rows_of(other)
    grad_block = swiglu_grads(core, x_own, x_other, dh_own, dh_other, replica, piece_rows)
    summed = lax.psum_scatter(grad_block, "z", scatter_dimension=0, tiled=True)
    replica_grad = summed.astype(f32)[None]

    outgoing = summed.reshape(slots, shard_width // LANES, LANES)
    incoming = lax.all_to_all(outgoing, "expert", split_axis=0, concat_axis=0, tiled=True)
    grads = lax.dot_general(
        slot_hot.astype(bf16),
        incoming.reshape(slots, shard_width),
        (((0,), (0,)), ((), ())),
        preferred_element_type=f32,
    )
    new_master, new_first, new_second = adamw_update(master, first_moment, second_moment, grads)
    return (new_master, new_first, new_second, replica_grad)


def solution(mesh):
    slots, dp = mesh.shape["expert"], mesh.shape["dp"]
    split = Mesh(
        mesh.devices.reshape(slots, dp // CORES, CORES), ("expert", "z", "c")
    )
    shard = ("z", "c", "expert")
    return jax.shard_map(
        local,
        mesh=split,
        in_specs=(
            P(shard, None),
            P(shard, None, None),
            P(shard, None),
            P(),
            P(None, shard),
            P(None, shard),
            P(None, shard),
        ),
        out_specs=(
            P(None, shard),
            P(None, shard),
            P(None, shard),
            P("expert", ("z", "c"), None),
        ),
        check_vma=False,
    )
```

```python
import functools

import jax
import jax.numpy as jnp
from jax import lax
from jax.experimental import pallas as pl
from jax.experimental.pallas import tpu as pltpu
from jax.sharding import Mesh, PartitionSpec as P


MOST = 5
LANES = 128
CORES = 2


beta_first = 0.9
beta_second = 0.95
learning_rate = 0.01
decay_rate = 0.1
epsilon = 1e-08
adam_steps = 20.0


def adamw_update(master, first_moment, second_moment, grads):
    new_first = beta_first * first_moment + (1.0 - beta_first) * grads
    new_second = beta_second * second_moment + (1.0 - beta_second) * grads * grads
    corr_first = 1.0 - beta_first**adam_steps
    corr_second = 1.0 - beta_second**adam_steps
    update = (
        new_first / corr_first / (jnp.sqrt(new_second / corr_second) + epsilon)
        + decay_rate * master
    )
    return (master - learning_rate * update, new_first, new_second)


def offset_of(block):
    return jnp.where(block % 2 == 1, (block + 1) // 2, -(block // 2))


def grads_kernel(planes, piece_rows, place, x_own, x_other, *refs):
    f32, bf16 = jnp.float32, jnp.bfloat16
    pieces, out, weights = refs[:planes], refs[planes], refs[planes + 1]
    units, width = weights.shape[0], weights.shape[1] // 2
    hidden = units * CORES
    for at, piece in enumerate(pieces):
        weights[at * piece_rows : (at + 1) * piece_rows, :] = piece[...]
    rows = x_own.shape[0]
    sources = rows // (MOST + 1)
    across = (((1,), (1,)), ((), ()))

    def iota(shape, dim):
        return lax.broadcasted_iota(jnp.int32, shape, dim)

    def hot(mask):
        return mask.astype(f32).astype(bf16)

    unit = iota((units, hidden), 0)
    block = unit // piece_rows
    plane = place[0] + offset_of(block) + planes
    plane = jnp.where(plane >= planes, plane - planes, plane)
    plane = jnp.where(plane >= planes, plane - planes, plane)
    column = (plane * CORES + place[1]) * piece_rows + unit - block * piece_rows
    choose = hot(iota((units, hidden), 1) == column)
    last = hot(iota((sources, rows), 1) == iota((sources, rows), 0) * (MOST + 1) + MOST)
    d_gates, d_ups = [], []
    for x_ref in (x_own, x_other):
        packed = jnp.dot(last, x_ref[:, : MOST * hidden], preferred_element_type=f32).astype(bf16)
        dh = jnp.zeros((units, rows), f32)
        for at in range(MOST):
            mine = packed[:, at * hidden : (at + 1) * hidden]
            mine = lax.dot_general(choose, mine, across, preferred_element_type=f32).astype(bf16)
            spread = hot(iota((sources, rows), 1) == iota((sources, rows), 0) * (MOST + 1) + at)
            dh += jnp.dot(mine, spread, preferred_element_type=f32)
        values = x_ref[...]
        gate = lax.dot_general(weights[:, :width], values, across, preferred_element_type=f32)
        up = lax.dot_general(weights[:, width:], values, across, preferred_element_type=f32)
        sig = jax.nn.sigmoid(gate)
        d_gates.append((dh * up * (sig * (1.0 + gate * (1.0 - sig)))).astype(bf16))
        d_ups.append((dh * (gate * sig)).astype(bf16))
    tile = 512
    for half, parts in enumerate((d_gates, d_ups)):
        for start in range(0, width, tile):
            cols = slice(start, start + tile)
            total = jnp.dot(parts[0], x_own[:, cols], preferred_element_type=f32)
            total += jnp.dot(parts[1], x_other[:, cols], preferred_element_type=f32)
            out[:, half * width + start : half * width + start + tile] = total.astype(bf16)


def swiglu_grads(planes, piece_rows, place, x_own, x_other, pieces):
    vmem = pl.BlockSpec(memory_space=pltpu.VMEM)
    shape = (planes * piece_rows, pieces[0].shape[1])
    flops = 8 * x_own.shape[0] * shape[0] * shape[1]
    return pl.pallas_call(
        functools.partial(grads_kernel, planes, piece_rows),
        out_shape=jax.ShapeDtypeStruct(shape, jnp.bfloat16),
        in_specs=[pl.BlockSpec(memory_space=pltpu.SMEM)] + [vmem] * (2 + planes),
        out_specs=vmem,
        scratch_shapes=[pltpu.VMEM(shape, jnp.bfloat16)],
        cost_estimate=pl.CostEstimate(flops=flops, bytes_accessed=8 << 20, transcendentals=0),
    )(place, x_own, x_other, *pieces)


def shift(value, planes, by):
    return lax.ppermute(value, "z", [(i, (i - by) % planes) for i in range(planes)])


def shift_by_core(value, planes, by):
    pairs = []
    for i in range(planes):
        pairs.append((i * CORES, (i - by) % planes * CORES))
        pairs.append((i * CORES + 1, (i + by) % planes * CORES + 1))
    return lax.ppermute(value, ("z", "c"), pairs)


def gather_planes(piece, planes):
    pieces = [piece]
    for by in range(1, planes // 2):
        pieces += [shift(piece, planes, by), shift(piece, planes, -by)]
    return pieces + [shift(piece, planes, planes // 2)]


def scatter_planes(blocks, planes, core):
    f32 = jnp.float32
    own, up1, down1, up2, down2, up3, down3, far = blocks
    more_up1, more_down1 = shift(up3, planes, -2), shift(down3, planes, 2)
    more_far = shift_by_core(far, planes, -2).astype(f32)
    first = core == 0

    def add(value, more):
        return (value.astype(f32) + more).astype(value.dtype)

    up1, down1 = add(up1, more_up1.astype(f32)), add(down1, more_down1.astype(f32))
    up2 = add(up2, jnp.where(first, more_far, 0.0))
    down2 = add(down2, jnp.where(first, 0.0, more_far))
    parts = [
        shift(up1, planes, -1),
        shift(down1, planes, 1),
        shift(up2, planes, -2),
        shift(down2, planes, 2),
    ]
    total = own.astype(f32)
    for part in parts:
        total = total + part.astype(f32)
    return total


def local(tokens, cotangent, expert_ids, placement, master, first_moment, second_moment):
    bf16, f32, i32 = jnp.bfloat16, jnp.float32, jnp.int32
    slots = lax.axis_size("expert")
    planes = lax.axis_size("z")
    source_index = lax.axis_index("expert")
    core = lax.axis_index("c")
    expert_count, shard_width = master.shape
    token_rows, width = tokens.shape
    top_count = expert_ids.shape[1]
    hidden = cotangent.shape[2]
    assigned = token_rows * top_count
    piece_rows = shard_width * slots // (2 * width)
    rows = slots * MOST
    expert_range = jnp.arange(expert_count, dtype=i32)
    slot_range = jnp.arange(slots, dtype=i32)

    slot_hot = placement[:, None] == expert_range[None, :]
    send_weight = jnp.dot(
        slot_hot.astype(bf16), master.astype(bf16), preferred_element_type=f32
    ).astype(bf16)
    send_weight = send_weight.reshape(slots, shard_width // LANES, LANES)
    recv_weight = lax.all_to_all(send_weight, "expert", split_axis=0, concat_axis=0, tiled=True)

    replicas = jnp.sum(slot_hot.astype(i32), axis=0)
    earlier_same = (slot_range[:, None] > slot_range[None, :]) & (
        placement[:, None] == placement[None, :]
    )
    slot_rank = jnp.sum(earlier_same.astype(i32), axis=1)
    wanted = jnp.mod(source_index, replicas)
    target_hot = slot_hot & (slot_rank[:, None] == wanted[None, :])
    target_slot = jnp.sum(jnp.where(target_hot, slot_range[:, None], 0), axis=0)
    flat_ids = expert_ids.reshape(assigned)
    expert_hot = flat_ids[:, None] == expert_range[None, :]
    copy_range = jnp.arange(assigned, dtype=i32)
    before = (copy_range[:, None] > copy_range[None, :]) & (flat_ids[:, None] == flat_ids[None, :])
    position = jnp.sum(before.astype(i32), axis=1)
    destination = jnp.sum(jnp.where(expert_hot, target_slot[None, :], 0), axis=1)
    send_row = destination * MOST + position
    row_match = jnp.arange(rows, dtype=i32)[:, None] == send_row[None, :]
    pick = row_match.astype(bf16)
    token_of = (copy_range[:, None] // top_count == jnp.arange(token_rows, dtype=i32)[None, :])
    token_pick = jnp.dot(pick, token_of.astype(bf16), preferred_element_type=f32).astype(bf16)
    send_x = jnp.dot(token_pick, tokens, preferred_element_type=f32).astype(bf16)
    send_dh = jnp.dot(
        pick, cotangent.reshape(assigned, hidden), preferred_element_type=f32
    ).astype(bf16)
    x_rows = MOST * width // LANES
    dh_rows = MOST * hidden // LANES
    spare = -(x_rows + dh_rows) % 16
    send = jnp.concatenate(
        [
            send_x.reshape(slots, x_rows, LANES),
            send_dh.reshape(slots, dh_rows, LANES),
            jnp.zeros((slots, spare, LANES), bf16),
        ],
        axis=1,
    )
    send, recv_weight = lax.optimization_barrier((send, recv_weight))
    recv = lax.all_to_all(send, "expert", split_axis=0, concat_axis=0, tiled=True)
    other = lax.ppermute(recv, "c", [(0, 1), (1, 0)])

    own_piece = recv_weight.reshape(piece_rows, 2 * width)
    pieces = gather_planes(own_piece, planes)

    group = MOST + 1
    place = jnp.stack([lax.axis_index("z"), core])
    grad_block = swiglu_grads(
        planes,
        piece_rows,
        place,
        recv.reshape(slots * group, width),
        other.reshape(slots * group, width),
        pieces,
    )
    blocks = [grad_block[k * piece_rows : (k + 1) * piece_rows] for k in range(planes)]
    summed = scatter_planes(blocks, planes, core)
    replica_grad = summed[None]

    outgoing = summed.astype(bf16).reshape(slots, shard_width // LANES, LANES)
    incoming = lax.all_to_all(outgoing, "expert", split_axis=0, concat_axis=0, tiled=True)
    incoming, replica_grad = lax.optimization_barrier((incoming, replica_grad))
    grads = lax.dot_general(
        slot_hot.astype(bf16),
        incoming.reshape(slots, shard_width),
        (((0,), (0,)), ((), ())),
        preferred_element_type=f32,
    )
    new_master, new_first, new_second = adamw_update(master, first_moment, second_moment, grads)
    return (new_master, new_first, new_second, replica_grad)


def solution(mesh):
    slots, dp = mesh.shape["expert"], mesh.shape["dp"]
    split = Mesh(
        mesh.devices.reshape(slots, dp // CORES, CORES), ("expert", "z", "c")
    )
    shard = ("z", "c", "expert")
    return jax.shard_map(
        local,
        mesh=split,
        in_specs=(
            P(shard, None),
            P(shard, None, None),
            P(shard, None),
            P(),
            P(None, shard),
            P(None, shard),
            P(None, shard),
        ),
        out_specs=(
            P(None, shard),
            P(None, shard),
            P(None, shard),
            P("expert", ("z", "c"), None),
        ),
        check_vma=False,
    )
```

```python
import functools

import jax
import jax.numpy as jnp
from jax import lax
from jax.experimental import pallas as pl
from jax.experimental.pallas import tpu as pltpu
from jax.sharding import Mesh, PartitionSpec as P


MOST = 5
LANES = 128
CORES = 2
FAR = 3


beta_first = 0.9
beta_second = 0.95
learning_rate = 0.01
decay_rate = 0.1
epsilon = 1e-08
adam_steps = 20.0


def adamw_update(master, first_moment, second_moment, grads):
    new_first = beta_first * first_moment + (1.0 - beta_first) * grads
    new_second = beta_second * second_moment + (1.0 - beta_second) * grads * grads
    corr_first = 1.0 - beta_first**adam_steps
    corr_second = 1.0 - beta_second**adam_steps
    update = (
        new_first / corr_first / (jnp.sqrt(new_second / corr_second) + epsilon)
        + decay_rate * master
    )
    return (master - learning_rate * update, new_first, new_second)


def offset_of(block, planes):
    return jnp.where(block % 2 == 1, (planes - 1 - block) // 2, -((planes - block) // 2))


def store_grads(outs, parts, rows_refs, piece_rows, width):
    tile = 512
    units = len(outs) * piece_rows
    for start in range(0, width, tile):
        cols = slice(start, start + tile)
        total = jnp.dot(parts[0], rows_refs[0][:, cols], preferred_element_type=jnp.float32)
        total += jnp.dot(parts[1], rows_refs[1][:, cols], preferred_element_type=jnp.float32)
        total = total.reshape(2, units, tile)
        for at, out in enumerate(outs):
            rows = slice(at * piece_rows, (at + 1) * piece_rows)
            out[:, start : start + tile] = total[0, rows].astype(jnp.bfloat16)
            out[:, width + start : width + start + tile] = total[1, rows].astype(jnp.bfloat16)


def far_kernel(planes, piece_rows, place, x_own, x_other, *refs):
    f32, bf16 = jnp.float32, jnp.bfloat16
    pieces, rest = refs[:planes], refs[planes:]
    outs, d_refs, weights = rest[:FAR], rest[FAR : FAR + CORES], rest[FAR + CORES]
    units, width = weights.shape[0] // 2, weights.shape[1]
    for at, piece in enumerate(pieces):
        lines = slice(at * piece_rows, (at + 1) * piece_rows)
        weights[lines, :] = piece[:, :width]
        lines = slice(units + at * piece_rows, units + (at + 1) * piece_rows)
        weights[lines, :] = piece[:, width:]
    hidden = units * CORES
    rows = x_own.shape[0]
    sources = rows // (MOST + 1)
    across = (((1,), (1,)), ((), ()))

    def iota(shape, dim):
        return lax.broadcasted_iota(jnp.int32, shape, dim)

    def hot(mask):
        return mask.astype(f32).astype(bf16)

    unit = iota((units, hidden), 0)
    block = unit // piece_rows
    plane = place[0] + offset_of(block, planes) + planes
    plane = jnp.where(plane >= planes, plane - planes, plane)
    plane = jnp.where(plane >= planes, plane - planes, plane)
    column = (plane * CORES + place[1]) * piece_rows + unit - block * piece_rows
    choose = hot(iota((units, hidden), 1) == column)
    last = hot(iota((sources, rows), 1) == iota((sources, rows), 0) * (MOST + 1) + MOST)
    far_units = FAR * piece_rows
    far_parts = []
    for x_ref, d_ref in zip((x_own, x_other), d_refs):
        packed = jnp.dot(last, x_ref[:, : MOST * hidden], preferred_element_type=f32).astype(bf16)
        dh = jnp.zeros((units, rows), f32)
        for at in range(MOST):
            mine = packed[:, at * hidden : (at + 1) * hidden]
            mine = lax.dot_general(choose, mine, across, preferred_element_type=f32).astype(bf16)
            spread = hot(iota((sources, rows), 1) == iota((sources, rows), 0) * (MOST + 1) + at)
            dh += jnp.dot(mine, spread, preferred_element_type=f32)
        both = lax.dot_general(weights[...], x_ref[...], across, preferred_element_type=f32)
        gate, up = both[:units], both[units:]
        sig = jax.nn.sigmoid(gate)
        d_gate = dh * up * (sig * (1.0 + gate * (1.0 - sig)))
        d_up = dh * (gate * sig)
        far_parts.append(
            jnp.concatenate([d_gate[:far_units], d_up[:far_units]], axis=0).astype(bf16)
        )
        d_ref[...] = jnp.concatenate([d_gate[far_units:], d_up[far_units:]], axis=0).astype(bf16)
    store_grads(outs, far_parts, (x_own, x_other), piece_rows, width)


def near_kernel(piece_rows, x_own, x_other, d_own, d_other, *outs):
    width = x_own.shape[1]
    store_grads(outs, (d_own[...], d_other[...]), (x_own, x_other), piece_rows, width)


def swiglu_grads(planes, piece_rows, place, x_own, x_other, pieces):
    bf16 = jnp.bfloat16
    vmem, smem = pl.BlockSpec(memory_space=pltpu.VMEM), pl.BlockSpec(memory_space=pltpu.SMEM)
    rows, width = x_own.shape
    units = planes * piece_rows
    near = planes - FAR
    block = jax.ShapeDtypeStruct((piece_rows, 2 * width), bf16)
    d_block = jax.ShapeDtypeStruct((2 * near * piece_rows, rows), bf16)
    dot_flops = 2 * CORES * rows * 2 * units * width
    *far_blocks, d_own, d_other = pl.pallas_call(
        functools.partial(far_kernel, planes, piece_rows),
        out_shape=[block] * FAR + [d_block] * CORES,
        in_specs=[smem] + [vmem] * (2 + planes),
        out_specs=[vmem] * (FAR + CORES),
        scratch_shapes=[pltpu.VMEM((2 * units, width), bf16)],
        cost_estimate=pl.CostEstimate(
            flops=dot_flops * (planes + FAR) // planes, bytes_accessed=6 << 20, transcendentals=0
        ),
    )(place, x_own, x_other, *pieces)
    near_blocks = pl.pallas_call(
        functools.partial(near_kernel, piece_rows),
        out_shape=[block] * near,
        in_specs=[vmem] * 4,
        out_specs=[vmem] * near,
        cost_estimate=pl.CostEstimate(
            flops=dot_flops * near // planes, bytes_accessed=4 << 20, transcendentals=0
        ),
    )(x_own, x_other, d_own, d_other)
    return far_blocks, near_blocks


def shift(value, planes, by):
    return lax.ppermute(value, "z", [(i, (i - by) % planes) for i in range(planes)])


def gather_planes(piece, planes):
    pieces = [shift(piece, planes, planes // 2)]
    for by in range(planes // 2 - 1, 0, -1):
        pieces += [shift(piece, planes, by), shift(piece, planes, -by)]
    return pieces + [piece]


def local(tokens, cotangent, expert_ids, placement, master, first_moment, second_moment):
    bf16, f32, i32 = jnp.bfloat16, jnp.float32, jnp.int32
    slots = lax.axis_size("expert")
    planes = lax.axis_size("z")
    source_index = lax.axis_index("expert")
    core = lax.axis_index("c")
    expert_count, shard_width = master.shape
    token_rows, width = tokens.shape
    top_count = expert_ids.shape[1]
    hidden = cotangent.shape[2]
    assigned = token_rows * top_count
    piece_rows = shard_width * slots // (2 * width)
    rows = slots * MOST
    expert_range = jnp.arange(expert_count, dtype=i32)
    slot_range = jnp.arange(slots, dtype=i32)

    slot_hot = placement[:, None] == expert_range[None, :]
    send_weight = jnp.dot(
        slot_hot.astype(bf16), master.astype(bf16), preferred_element_type=f32
    ).astype(bf16)
    send_weight = send_weight.reshape(slots, shard_width // LANES, LANES)
    recv_weight = lax.all_to_all(send_weight, "expert", split_axis=0, concat_axis=0, tiled=True)

    replicas = jnp.sum(slot_hot.astype(i32), axis=0)
    earlier_same = (slot_range[:, None] > slot_range[None, :]) & (
        placement[:, None] == placement[None, :]
    )
    slot_rank = jnp.sum(earlier_same.astype(i32), axis=1)
    wanted = jnp.mod(source_index, replicas)
    target_hot = slot_hot & (slot_rank[:, None] == wanted[None, :])
    target_slot = jnp.sum(jnp.where(target_hot, slot_range[:, None], 0), axis=0)
    flat_ids = expert_ids.reshape(assigned)
    expert_hot = flat_ids[:, None] == expert_range[None, :]
    copy_range = jnp.arange(assigned, dtype=i32)
    before = (copy_range[:, None] > copy_range[None, :]) & (flat_ids[:, None] == flat_ids[None, :])
    position = jnp.sum(before.astype(i32), axis=1)
    destination = jnp.sum(jnp.where(expert_hot, target_slot[None, :], 0), axis=1)
    send_row = destination * MOST + position
    row_match = jnp.arange(rows, dtype=i32)[:, None] == send_row[None, :]
    pick = row_match.astype(bf16)
    token_of = (copy_range[:, None] // top_count == jnp.arange(token_rows, dtype=i32)[None, :])
    token_pick = jnp.dot(pick, token_of.astype(bf16), preferred_element_type=f32).astype(bf16)
    send_x = jnp.dot(token_pick, tokens, preferred_element_type=f32).astype(bf16)
    send_dh = jnp.dot(
        pick, cotangent.reshape(assigned, hidden), preferred_element_type=f32
    ).astype(bf16)
    x_rows = MOST * width // LANES
    dh_rows = MOST * hidden // LANES
    spare = -(x_rows + dh_rows) % 16
    send = jnp.concatenate(
        [
            send_x.reshape(slots, x_rows, LANES),
            send_dh.reshape(slots, dh_rows, LANES),
            jnp.zeros((slots, spare, LANES), bf16),
        ],
        axis=1,
    )
    send, recv_weight = lax.optimization_barrier((send, recv_weight))
    recv = lax.all_to_all(send, "expert", split_axis=0, concat_axis=0, tiled=True)
    other = lax.ppermute(recv, "c", [(0, 1), (1, 0)])

    own_piece = recv_weight.reshape(piece_rows, 2 * width)
    pieces = gather_planes(own_piece, planes)

    group = MOST + 1
    place = jnp.stack([lax.axis_index("z"), core])
    far_blocks, near_blocks = swiglu_grads(
        planes,
        piece_rows,
        place,
        recv.reshape(slots * group, width),
        other.reshape(slots * group, width),
        pieces,
    )
    parts = [shift(far_blocks[0], planes, planes // 2)]
    parts += [shift(far_blocks[1], planes, -3), shift(far_blocks[2], planes, 3)]
    parts += [shift(near_blocks[0], planes, -2), shift(near_blocks[1], planes, 2)]
    parts += [shift(near_blocks[2], planes, -1), shift(near_blocks[3], planes, 1)]
    summed = near_blocks[4].astype(f32)
    for part in parts:
        summed = summed + part.astype(f32)
    replica_grad = summed[None]

    outgoing = summed.astype(bf16).reshape(slots, shard_width // LANES, LANES)
    incoming = lax.all_to_all(outgoing, "expert", split_axis=0, concat_axis=0, tiled=True)
    incoming, replica_grad = lax.optimization_barrier((incoming, replica_grad))
    grads = lax.dot_general(
        slot_hot.astype(bf16),
        incoming.reshape(slots, shard_width),
        (((0,), (0,)), ((), ())),
        preferred_element_type=f32,
    )
    new_master, new_first, new_second = adamw_update(master, first_moment, second_moment, grads)
    return (new_master, new_first, new_second, replica_grad)


def solution(mesh):
    slots, dp = mesh.shape["expert"], mesh.shape["dp"]
    split = Mesh(
        mesh.devices.reshape(slots, dp // CORES, CORES), ("expert", "z", "c")
    )
    shard = ("z", "c", "expert")
    return jax.shard_map(
        local,
        mesh=split,
        in_specs=(
            P(shard, None),
            P(shard, None, None),
            P(shard, None),
            P(),
            P(None, shard),
            P(None, shard),
            P(None, shard),
        ),
        out_specs=(
            P(None, shard),
            P(None, shard),
            P(None, shard),
            P("expert", ("z", "c"), None),
        ),
        check_vma=False,
    )
```

```python
import functools

import jax
import jax.numpy as jnp
from jax import lax
from jax.experimental import pallas as pl
from jax.experimental.pallas import tpu as pltpu
from jax.sharding import Mesh, PartitionSpec as P


MOST = 5
LANES = 128
CORES = 2
FAR = 3
GRANT = 24 << 20


beta_first = 0.9
beta_second = 0.95
learning_rate = 0.01
decay_rate = 0.1
epsilon = 1e-08
adam_steps = 20.0


def adamw_update(master, first_moment, second_moment, grads):
    new_first = beta_first * first_moment + (1.0 - beta_first) * grads
    new_second = beta_second * second_moment + (1.0 - beta_second) * grads * grads
    corr_first = 1.0 - beta_first**adam_steps
    corr_second = 1.0 - beta_second**adam_steps
    update = (
        new_first / corr_first / (jnp.sqrt(new_second / corr_second) + epsilon)
        + decay_rate * master
    )
    return (master - learning_rate * update, new_first, new_second)


def offset_of(block, planes):
    return jnp.where(block % 2 == 1, (planes - 1 - block) // 2, -((planes - block) // 2))


def store_grads(outs, parts, rows_refs, piece_rows, width):
    tile = 512
    units = len(outs) * piece_rows
    for start in range(0, width, tile):
        cols = slice(start, start + tile)
        total = jnp.dot(parts[0], rows_refs[0][:, cols], preferred_element_type=jnp.float32)
        total += jnp.dot(parts[1], rows_refs[1][:, cols], preferred_element_type=jnp.float32)
        total = total.reshape(2, units, tile)
        for at, out in enumerate(outs):
            rows = slice(at * piece_rows, (at + 1) * piece_rows)
            out[:, start : start + tile] = total[0, rows].astype(jnp.bfloat16)
            out[:, width + start : width + start + tile] = total[1, rows].astype(jnp.bfloat16)


def grads_kernel(planes, piece_rows, first_block, count, place, x_own, x_other, *refs):
    f32, bf16 = jnp.float32, jnp.bfloat16
    pieces, outs, weights = refs[:count], refs[count : 2 * count], refs[2 * count]
    units, width = weights.shape[0] // 2, weights.shape[1]
    for at, piece in enumerate(pieces):
        lines = slice(at * piece_rows, (at + 1) * piece_rows)
        weights[lines, :] = piece[:, :width]
        lines = slice(units + at * piece_rows, units + (at + 1) * piece_rows)
        weights[lines, :] = piece[:, width:]
    hidden = planes * piece_rows * CORES
    rows = x_own.shape[0]
    sources = rows // (MOST + 1)
    across = (((1,), (1,)), ((), ()))

    def iota(shape, dim):
        return lax.broadcasted_iota(jnp.int32, shape, dim)

    def hot(mask):
        return mask.astype(f32).astype(bf16)

    unit = iota((units, hidden), 0)
    block = unit // piece_rows
    plane = place[0] + offset_of(block + first_block, planes) + planes
    plane = jnp.where(plane >= planes, plane - planes, plane)
    plane = jnp.where(plane >= planes, plane - planes, plane)
    column = (plane * CORES + place[1]) * piece_rows + unit - block * piece_rows
    choose = hot(iota((units, hidden), 1) == column)
    last = hot(iota((sources, rows), 1) == iota((sources, rows), 0) * (MOST + 1) + MOST)
    parts = []
    for x_ref in (x_own, x_other):
        packed = jnp.dot(last, x_ref[:, : MOST * hidden], preferred_element_type=f32).astype(bf16)
        dh = jnp.zeros((units, rows), f32)
        for at in range(MOST):
            mine = packed[:, at * hidden : (at + 1) * hidden]
            mine = lax.dot_general(choose, mine, across, preferred_element_type=f32).astype(bf16)
            spread = hot(iota((sources, rows), 1) == iota((sources, rows), 0) * (MOST + 1) + at)
            dh += jnp.dot(mine, spread, preferred_element_type=f32)
        both = lax.dot_general(weights[...], x_ref[...], across, preferred_element_type=f32)
        gate, up = both[:units], both[units:]
        sig = jax.nn.sigmoid(gate)
        d_gate = dh * up * (sig * (1.0 + gate * (1.0 - sig)))
        d_up = dh * (gate * sig)
        parts.append(jnp.concatenate([d_gate, d_up], axis=0).astype(bf16))
    store_grads(outs, parts, (x_own, x_other), piece_rows, width)


def swiglu_grads(planes, piece_rows, first_block, place, x_own, x_other, pieces):
    bf16 = jnp.bfloat16
    vmem, smem = pl.BlockSpec(memory_space=pltpu.VMEM), pl.BlockSpec(memory_space=pltpu.SMEM)
    rows, width = x_own.shape
    count = len(pieces)
    units = count * piece_rows
    block = jax.ShapeDtypeStruct((piece_rows, 2 * width), bf16)
    return pl.pallas_call(
        functools.partial(grads_kernel, planes, piece_rows, first_block, count),
        out_shape=[block] * count,
        in_specs=[smem] + [vmem] * (2 + count),
        out_specs=[vmem] * count,
        scratch_shapes=[pltpu.VMEM((2 * units, width), bf16)],
        compiler_params=pltpu.CompilerParams(vmem_limit_bytes=GRANT),
        cost_estimate=pl.CostEstimate(
            flops=8 * CORES * rows * units * width, bytes_accessed=5 << 20, transcendentals=0
        ),
    )(place, x_own, x_other, *pieces)


def shift(value, planes, by):
    return lax.ppermute(value, "z", [(i, (i - by) % planes) for i in range(planes)])


def shift_by_core(value, planes, by):
    pairs = []
    for i in range(planes):
        pairs.append((i * CORES, (i - by) % planes * CORES))
        pairs.append((i * CORES + 1, (i + by) % planes * CORES + 1))
    return lax.ppermute(value, ("z", "c"), pairs)


def gather_planes(piece, planes):
    pieces = [shift(piece, planes, planes // 2)]
    by = planes // 2 - 1
    pieces += [shift(piece, planes, by), shift(piece, planes, -by)]
    for by in range(planes // 2 - 2, 0, -1):
        pieces += [shift(piece, planes, by), shift(piece, planes, -by)]
    return pieces + [piece]


def local(tokens, cotangent, expert_ids, placement, master, first_moment, second_moment):
    bf16, f32, i32 = jnp.bfloat16, jnp.float32, jnp.int32
    slots = lax.axis_size("expert")
    planes = lax.axis_size("z")
    source_index = lax.axis_index("expert")
    core = lax.axis_index("c")
    expert_count, shard_width = master.shape
    token_rows, width = tokens.shape
    top_count = expert_ids.shape[1]
    hidden = cotangent.shape[2]
    assigned = token_rows * top_count
    piece_rows = shard_width * slots // (2 * width)
    rows = slots * MOST
    expert_range = jnp.arange(expert_count, dtype=i32)
    slot_range = jnp.arange(slots, dtype=i32)

    slot_hot = placement[:, None] == expert_range[None, :]
    send_weight = jnp.dot(
        slot_hot.astype(bf16), master.astype(bf16), preferred_element_type=f32
    ).astype(bf16)
    send_weight = send_weight.reshape(slots, shard_width // LANES, LANES)
    recv_weight = lax.all_to_all(send_weight, "expert", split_axis=0, concat_axis=0, tiled=True)

    replicas = jnp.sum(slot_hot.astype(i32), axis=0)
    earlier_same = (slot_range[:, None] > slot_range[None, :]) & (
        placement[:, None] == placement[None, :]
    )
    slot_rank = jnp.sum(earlier_same.astype(i32), axis=1)
    wanted = jnp.mod(source_index, replicas)
    target_hot = slot_hot & (slot_rank[:, None] == wanted[None, :])
    target_slot = jnp.sum(jnp.where(target_hot, slot_range[:, None], 0), axis=0)
    flat_ids = expert_ids.reshape(assigned)
    expert_hot = flat_ids[:, None] == expert_range[None, :]
    copy_range = jnp.arange(assigned, dtype=i32)
    before = (copy_range[:, None] > copy_range[None, :]) & (flat_ids[:, None] == flat_ids[None, :])
    position = jnp.sum(before.astype(i32), axis=1)
    destination = jnp.sum(jnp.where(expert_hot, target_slot[None, :], 0), axis=1)
    send_row = destination * MOST + position
    row_match = jnp.arange(rows, dtype=i32)[:, None] == send_row[None, :]
    pick = row_match.astype(bf16)
    token_of = (copy_range[:, None] // top_count == jnp.arange(token_rows, dtype=i32)[None, :])
    token_pick = jnp.dot(pick, token_of.astype(bf16), preferred_element_type=f32).astype(bf16)
    send_x = jnp.dot(token_pick, tokens, preferred_element_type=f32).astype(bf16)
    send_dh = jnp.dot(
        pick, cotangent.reshape(assigned, hidden), preferred_element_type=f32
    ).astype(bf16)
    x_rows = MOST * width // LANES
    dh_rows = MOST * hidden // LANES
    spare = -(x_rows + dh_rows) % 16
    send = jnp.concatenate(
        [
            send_x.reshape(slots, x_rows, LANES),
            send_dh.reshape(slots, dh_rows, LANES),
            jnp.zeros((slots, spare, LANES), bf16),
        ],
        axis=1,
    )
    send, recv_weight = lax.optimization_barrier((send, recv_weight))
    recv = lax.all_to_all(send, "expert", split_axis=0, concat_axis=0, tiled=True)
    other = lax.ppermute(recv, "c", [(0, 1), (1, 0)])

    own_piece = recv_weight.reshape(piece_rows, 2 * width)
    pieces = gather_planes(own_piece, planes)

    group = MOST + 1
    place = jnp.stack([lax.axis_index("z"), core])
    x_own = recv.reshape(slots * group, width)
    x_other = other.reshape(slots * group, width)
    far = swiglu_grads(planes, piece_rows, 0, place, x_own, x_other, pieces[:FAR])
    relayed = shift_by_core(far[0], planes, -2)
    parts = [shift(far[1], planes, -3), shift(far[2], planes, 3)]
    near = swiglu_grads(planes, piece_rows, FAR, place, x_own, x_other, pieces[FAR:])
    up2, down2, up1, down1, own = near
    more = relayed.astype(f32)
    up2 = (up2.astype(f32) + jnp.where(core == 0, more, 0.0)).astype(bf16)
    down2 = (down2.astype(f32) + jnp.where(core == 0, 0.0, more)).astype(bf16)
    parts += [shift(up2, planes, -2), shift(down2, planes, 2)]
    parts += [shift(up1, planes, -1), shift(down1, planes, 1)]
    summed = own.astype(f32)
    for part in parts:
        summed = summed + part.astype(f32)
    replica_grad = summed[None]

    outgoing = summed.astype(bf16).reshape(slots, shard_width // LANES, LANES)
    incoming = lax.all_to_all(outgoing, "expert", split_axis=0, concat_axis=0, tiled=True)
    incoming, replica_grad = lax.optimization_barrier((incoming, replica_grad))
    grads = lax.dot_general(
        slot_hot.astype(bf16),
        incoming.reshape(slots, shard_width),
        (((0,), (0,)), ((), ())),
        preferred_element_type=f32,
    )
    new_master, new_first, new_second = adamw_update(master, first_moment, second_moment, grads)
    return (new_master, new_first, new_second, replica_grad)


def solution(mesh):
    slots, dp = mesh.shape["expert"], mesh.shape["dp"]
    split = Mesh(
        mesh.devices.reshape(slots, dp // CORES, CORES), ("expert", "z", "c")
    )
    shard = ("z", "c", "expert")
    return jax.shard_map(
        local,
        mesh=split,
        in_specs=(
            P(shard, None),
            P(shard, None, None),
            P(shard, None),
            P(),
            P(None, shard),
            P(None, shard),
            P(None, shard),
        ),
        out_specs=(
            P(None, shard),
            P(None, shard),
            P(None, shard),
            P("expert", ("z", "c"), None),
        ),
        check_vma=False,
    )
```

```python
import functools

import jax
import jax.numpy as jnp
from jax import lax
from jax.experimental import pallas as pl
from jax.experimental.pallas import tpu as pltpu
from jax.sharding import Mesh, PartitionSpec as P


MOST = 5
LANES = 128
CORES = 2
FAR = 3
GRANT = 24 << 20


beta_first = 0.9
beta_second = 0.95
learning_rate = 0.01
decay_rate = 0.1
epsilon = 1e-08
adam_steps = 20.0


def adamw_update(master, first_moment, second_moment, grads):
    new_first = beta_first * first_moment + (1.0 - beta_first) * grads
    new_second = beta_second * second_moment + (1.0 - beta_second) * grads * grads
    corr_first = 1.0 - beta_first**adam_steps
    corr_second = 1.0 - beta_second**adam_steps
    update = (
        new_first / corr_first / (jnp.sqrt(new_second / corr_second) + epsilon)
        + decay_rate * master
    )
    return (master - learning_rate * update, new_first, new_second)


def offset_of(block, planes):
    return jnp.where(block % 2 == 1, (planes - 1 - block) // 2, -((planes - block) // 2))


def store_grads(outs, parts, rows_refs, units, width):
    tile = 512
    for start in range(0, width, tile):
        cols = slice(start, start + tile)
        total = jnp.dot(parts[0], rows_refs[0][:, cols], preferred_element_type=jnp.float32)
        total += jnp.dot(parts[1], rows_refs[1][:, cols], preferred_element_type=jnp.float32)
        total = total.reshape(2, units, tile)
        for out, lines in outs:
            to = 0
            for first, end in lines:
                rows = slice(to, to + end - first)
                out[rows, start : start + tile] = total[0, first:end].astype(jnp.bfloat16)
                more = slice(width + start, width + start + tile)
                out[rows, more] = total[1, first:end].astype(jnp.bfloat16)
                to += end - first


def grads_kernel(planes, piece_rows, first_block, count, lines_of, place, x_own, x_other, *refs):
    f32, bf16 = jnp.float32, jnp.bfloat16
    pieces, outs, weights = refs[:count], refs[count:-1], refs[-1]
    units, width = weights.shape[0] // 2, weights.shape[1]
    for at, piece in enumerate(pieces):
        lines = slice(at * piece_rows, (at + 1) * piece_rows)
        weights[lines, :] = piece[:, :width]
        lines = slice(units + at * piece_rows, units + (at + 1) * piece_rows)
        weights[lines, :] = piece[:, width:]
    hidden = planes * piece_rows * CORES
    rows = x_own.shape[0]
    sources = rows // (MOST + 1)
    across = (((1,), (1,)), ((), ()))

    def iota(shape, dim):
        return lax.broadcasted_iota(jnp.int32, shape, dim)

    def hot(mask):
        return mask.astype(f32).astype(bf16)

    unit = iota((units, hidden), 0)
    block = unit // piece_rows
    plane = place[0] + offset_of(block + first_block, planes) + planes
    plane = jnp.where(plane >= planes, plane - planes, plane)
    plane = jnp.where(plane >= planes, plane - planes, plane)
    column = (plane * CORES + place[1]) * piece_rows + unit - block * piece_rows
    choose = hot(iota((units, hidden), 1) == column)
    last = hot(iota((sources, rows), 1) == iota((sources, rows), 0) * (MOST + 1) + MOST)
    parts = []
    for x_ref in (x_own, x_other):
        packed = jnp.dot(last, x_ref[:, : MOST * hidden], preferred_element_type=f32).astype(bf16)
        dh = jnp.zeros((units, rows), f32)
        for at in range(MOST):
            mine = packed[:, at * hidden : (at + 1) * hidden]
            mine = lax.dot_general(choose, mine, across, preferred_element_type=f32).astype(bf16)
            spread = hot(iota((sources, rows), 1) == iota((sources, rows), 0) * (MOST + 1) + at)
            dh += jnp.dot(mine, spread, preferred_element_type=f32)
        both = lax.dot_general(weights[...], x_ref[...], across, preferred_element_type=f32)
        gate, up = both[:units], both[units:]
        sig = jax.nn.sigmoid(gate)
        d_gate = dh * up * (sig * (1.0 + gate * (1.0 - sig)))
        d_up = dh * (gate * sig)
        parts.append(jnp.concatenate([d_gate, d_up], axis=0).astype(bf16))
    store_grads(list(zip(outs, lines_of)), parts, (x_own, x_other), units, width)


def swiglu_grads(planes, piece_rows, first_block, place, x_own, x_other, pieces, lines_of):
    bf16 = jnp.bfloat16
    vmem, smem = pl.BlockSpec(memory_space=pltpu.VMEM), pl.BlockSpec(memory_space=pltpu.SMEM)
    rows, width = x_own.shape
    count = len(pieces)
    units = count * piece_rows
    blocks = [
        jax.ShapeDtypeStruct((sum(end - first for first, end in lines), 2 * width), bf16)
        for lines in lines_of
    ]
    return pl.pallas_call(
        functools.partial(grads_kernel, planes, piece_rows, first_block, count, lines_of),
        out_shape=blocks,
        in_specs=[smem] + [vmem] * (2 + count),
        out_specs=[vmem] * len(blocks),
        scratch_shapes=[pltpu.VMEM((2 * units, width), bf16)],
        compiler_params=pltpu.CompilerParams(vmem_limit_bytes=GRANT),
        cost_estimate=pl.CostEstimate(
            flops=8 * CORES * rows * units * width, bytes_accessed=5 << 20, transcendentals=0
        ),
    )(place, x_own, x_other, *pieces)


def shift(value, planes, by):
    return lax.ppermute(value, "z", [(i, (i - by) % planes) for i in range(planes)])


def gather_planes(piece, planes):
    pieces = [shift(piece, planes, planes // 2)]
    by = planes // 2 - 1
    pieces += [shift(piece, planes, by), shift(piece, planes, -by)]
    for by in range(planes // 2 - 2, 0, -1):
        pieces += [shift(piece, planes, by), shift(piece, planes, -by)]
    return pieces + [piece]


def local(tokens, cotangent, expert_ids, placement, master, first_moment, second_moment):
    bf16, f32, i32 = jnp.bfloat16, jnp.float32, jnp.int32
    slots = lax.axis_size("expert")
    planes = lax.axis_size("z")
    source_index = lax.axis_index("expert")
    core = lax.axis_index("c")
    expert_count, shard_width = master.shape
    token_rows, width = tokens.shape
    top_count = expert_ids.shape[1]
    hidden = cotangent.shape[2]
    assigned = token_rows * top_count
    piece_rows = shard_width * slots // (2 * width)
    rows = slots * MOST
    expert_range = jnp.arange(expert_count, dtype=i32)
    slot_range = jnp.arange(slots, dtype=i32)

    slot_hot = placement[:, None] == expert_range[None, :]
    send_weight = jnp.dot(
        slot_hot.astype(bf16), master.astype(bf16), preferred_element_type=f32
    ).astype(bf16)
    send_weight = send_weight.reshape(slots, shard_width // LANES, LANES)
    recv_weight = lax.all_to_all(send_weight, "expert", split_axis=0, concat_axis=0, tiled=True)

    replicas = jnp.sum(slot_hot.astype(i32), axis=0)
    earlier_same = (slot_range[:, None] > slot_range[None, :]) & (
        placement[:, None] == placement[None, :]
    )
    slot_rank = jnp.sum(earlier_same.astype(i32), axis=1)
    wanted = jnp.mod(source_index, replicas)
    target_hot = slot_hot & (slot_rank[:, None] == wanted[None, :])
    target_slot = jnp.sum(jnp.where(target_hot, slot_range[:, None], 0), axis=0)
    flat_ids = expert_ids.reshape(assigned)
    expert_hot = flat_ids[:, None] == expert_range[None, :]
    copy_range = jnp.arange(assigned, dtype=i32)
    before = (copy_range[:, None] > copy_range[None, :]) & (flat_ids[:, None] == flat_ids[None, :])
    position = jnp.sum(before.astype(i32), axis=1)
    destination = jnp.sum(jnp.where(expert_hot, target_slot[None, :], 0), axis=1)
    send_row = destination * MOST + position
    row_match = jnp.arange(rows, dtype=i32)[:, None] == send_row[None, :]
    pick = row_match.astype(bf16)
    token_of = (copy_range[:, None] // top_count == jnp.arange(token_rows, dtype=i32)[None, :])
    token_pick = jnp.dot(pick, token_of.astype(bf16), preferred_element_type=f32).astype(bf16)
    send_x = jnp.dot(token_pick, tokens, preferred_element_type=f32).astype(bf16)
    send_dh = jnp.dot(
        pick, cotangent.reshape(assigned, hidden), preferred_element_type=f32
    ).astype(bf16)
    x_rows = MOST * width // LANES
    dh_rows = MOST * hidden // LANES
    spare = -(x_rows + dh_rows) % 16
    send = jnp.concatenate(
        [
            send_x.reshape(slots, x_rows, LANES),
            send_dh.reshape(slots, dh_rows, LANES),
            jnp.zeros((slots, spare, LANES), bf16),
        ],
        axis=1,
    )
    send, recv_weight = lax.optimization_barrier((send, recv_weight))
    recv = lax.all_to_all(send, "expert", split_axis=0, concat_axis=0, tiled=True)
    other = lax.ppermute(recv, "c", [(0, 1), (1, 0)])

    own_piece = recv_weight.reshape(piece_rows, 2 * width)
    pieces = gather_planes(own_piece, planes)

    group = MOST + 1
    place = jnp.stack([lax.axis_index("z"), core])
    x_own = recv.reshape(slots * group, width)
    x_other = other.reshape(slots * group, width)
    part = piece_rows // 3 * 2
    far_lines = (
        ((piece_rows, 2 * piece_rows), (0, part)),
        ((2 * piece_rows, 3 * piece_rows), (part, piece_rows)),
    )
    near_lines = tuple(((k * piece_rows, (k + 1) * piece_rows),) for k in range(planes - FAR))
    above, below = swiglu_grads(
        planes, piece_rows, 0, place, x_own, x_other, pieces[:FAR], far_lines
    )
    above, below = shift(above, planes, -2), shift(below, planes, 2)
    near = swiglu_grads(planes, piece_rows, FAR, place, x_own, x_other, pieces[FAR:], near_lines)
    up2, down2, up1, down1, own = near
    above, below = above.astype(f32), below.astype(f32)
    over = jnp.pad(above[piece_rows:], ((0, piece_rows - part), (0, 0)))
    under = jnp.pad(below[piece_rows:], ((part, 0), (0, 0)))
    up2 = (up2.astype(f32) + over).astype(bf16)
    down2 = (down2.astype(f32) + under).astype(bf16)
    up1 = (up1.astype(f32) + above[:piece_rows]).astype(bf16)
    down1 = (down1.astype(f32) + below[:piece_rows]).astype(bf16)
    parts = [shift(up2, planes, -2), shift(down2, planes, 2)]
    parts += [shift(up1, planes, -1), shift(down1, planes, 1)]
    summed = own.astype(f32)
    for part in parts:
        summed = summed + part.astype(f32)
    replica_grad = summed[None]

    outgoing = summed.astype(bf16).reshape(slots, shard_width // LANES, LANES)
    incoming = lax.all_to_all(outgoing, "expert", split_axis=0, concat_axis=0, tiled=True)
    incoming, replica_grad = lax.optimization_barrier((incoming, replica_grad))
    grads = lax.dot_general(
        slot_hot.astype(bf16),
        incoming.reshape(slots, shard_width),
        (((0,), (0,)), ((), ())),
        preferred_element_type=f32,
    )
    new_master, new_first, new_second = adamw_update(master, first_moment, second_moment, grads)
    return (new_master, new_first, new_second, replica_grad)


def solution(mesh):
    slots, dp = mesh.shape["expert"], mesh.shape["dp"]
    split = Mesh(
        mesh.devices.reshape(slots, dp // CORES, CORES), ("expert", "z", "c")
    )
    shard = ("z", "c", "expert")
    return jax.shard_map(
        local,
        mesh=split,
        in_specs=(
            P(shard, None),
            P(shard, None, None),
            P(shard, None),
            P(),
            P(None, shard),
            P(None, shard),
            P(None, shard),
        ),
        out_specs=(
            P(None, shard),
            P(None, shard),
            P(None, shard),
            P("expert", ("z", "c"), None),
        ),
        check_vma=False,
    )
```
